32 devices in a mesh: rows: 8 (over y, x, core), cols: 4 (over z).
Axes of the slice: x: 2, y: 2, z: 4, core: 2. Of those that a mesh axis runs over, the one named last changes fastest.
Arguments:
- gradient: bfloat16 [32, 16384], P('rows', 'cols'), may hold values from -6 to 6
- basis: float32 [16384, 16384], P('cols', 'rows'), may hold values from -0.046875 to 0.046875
- moment: float32 [32, 16384], P('cols', 'rows'), may hold values from -2 to 2
- second: float32 [32, 16384], P('cols', 'rows'), may hold values from 0.05 to 2
Outputs:
- update: float32 [32, 16384], P('rows', 'cols')
- moment_new: float32 [32, 16384], P('cols', 'rows')
- second_new: float32 [32, 16384], P('cols', 'rows')
The draws below stay inside these ranges and needn't reach their ends.
All inputs are finite; a program needn't handle non-finite values.
Results may differ from the reference program's by a relative error of at most 0.0003.
Values may be sent and summed in bfloat16 or wider, within the bound.
No kernel may reach another device: no remote copies, remote signals or barrier semaphores. Data moves between devices by JAX's collectives and lax.ppermute only.
A program may use at most 64 MiB of HBM per device.

```python
import math
import jax
import jax.numpy as jnp
from jax import lax

D = 16384
M = 32


def levels(own_key, shape, split, low, largest):
    def one(position, shards_of):
        heights = jax.random.uniform(jax.random.fold_in(jax.random.fold_in(own_key, 6), position), (shards_of,), jnp.float32, low / len(split), largest / len(split))
        return jnp.repeat(jnp.exp(heights), shape[position] // shards_of).reshape((-1,) + (1,) * (len(shape) - position - 1))

    gain = one(*split[0])
    for cut in split[1:]:
        gain = gain * one(*cut)
    return gain


def gaussian(own_key, extent, scale, limit, shards=(), kind=jnp.bfloat16):
    array = scale * jax.random.normal(own_key, extent, jnp.float32)
    if shards:
        array = array * levels(own_key, extent, shards, -0.22, 0.18)
    return jnp.clip(array, -limit, limit).astype(kind)


def setup_inputs(seed: int = 0) -> dict:
    key_of = jax.random.split(jax.random.key(seed), 5)
    return {
        "gradient": gaussian(key_of[0], (M, D), 1.0, 6.0, ((0, 8), (1, 4))),
        "basis": gaussian(key_of[1], (D, D), D ** -0.5, 0.046875, ((0, 4), (1, 8)), jnp.float32),
        "moment": gaussian(key_of[2], (M, D), 0.3, 2.0, ((0, 4), (1, 8)), jnp.float32),
        "second": jnp.clip(jnp.exp(math.log(2.0) - 3.6888794 * jax.random.uniform(key_of[3], (M, D), jnp.float32) ** levels(key_of[3], (M, D), ((0, 4), (1, 8)), -0.2, 0.2)), 0.05, 2.0),
    }


def reference(gradient, basis, moment, second):
    widened = gradient.astype(jnp.float32)
    rotated = jnp.dot(widened, basis, precision=lax.Precision.HIGHEST, preferred_element_type=jnp.float32)
    moment_new = 0.9 * moment + 0.1 * rotated
    second_new = 0.95 * second + 0.05 * rotated * rotated
    normed = moment_new / (1.0 - 0.9 ** 10) / (jnp.sqrt(second_new / (1.0 - 0.95 ** 10)) + 1e-08)
    update = lax.dot_general(normed, basis, (((1,), (1,)), ((), ())), precision=lax.Precision.HIGHEST, preferred_element_type=jnp.float32)
    return (update, moment_new, second_new)
```

```python
import functools

import jax
import jax.numpy as jnp
from jax import lax
from jax.experimental import pallas as pl
from jax.experimental.pallas import tpu as pltpu
from jax.sharding import PartitionSpec as P

F32, BF16 = jnp.float32, jnp.bfloat16
WHOLE = pl.BlockSpec(memory_space=pltpu.VMEM)
TRANSPOSED = (((1,), (1,)), ((), ()))


def adam_moments(moment, second, rotated):
    moment_new = 0.9 * moment + 0.1 * rotated
    second_new = 0.95 * second + 0.05 * rotated * rotated
    normed = moment_new / (1.0 - 0.9**10) / (jnp.sqrt(second_new / (1.0 - 0.95**10)) + 1e-08)
    return (moment_new, second_new, normed)


def split(x):
    high = x.astype(BF16)
    return high, (x - high.astype(F32)).astype(BF16)


def tile(size, most):
    while size % most:
        most //= 2
    return most


def call(kernel, outs, *args, limit=20 << 20):
    return pl.pallas_call(
        kernel,
        out_shape=outs,
        in_specs=[WHOLE] * len(args),
        out_specs=jax.tree.map(lambda _: WHOLE, outs),
        compiler_params=pltpu.CompilerParams(vmem_limit_bytes=limit),
    )(*args)


def f32(*shape):
    return jax.ShapeDtypeStruct(shape, F32)


def rotate_kernel(g_ref, b_ref, *outs):
    depth, width = b_ref.shape
    rows = g_ref.shape[0] * g_ref.shape[1]
    n = len(outs)
    kt, nt = tile(depth, 1024), tile(width, 256)
    me = lax.axis_index("cols")

    def columns(j, _):
        cs = pl.ds(pl.multiple_of(j * nt, nt), nt)

        def inner(k, total):
            ks = pl.ds(pl.multiple_of(k * kt, kt), kt)
            g = g_ref[:, :, ks].astype(F32).reshape(rows, kt).astype(BF16)
            high, low = split(b_ref[ks, cs])
            return total + jnp.dot(g, high, preferred_element_type=F32) + jnp.dot(g, low, preferred_element_type=F32)

        total = lax.fori_loop(0, depth // kt, inner, jnp.zeros((rows, nt), F32))
        blocks = total.reshape(n, rows // n, nt)
        for s, out in enumerate(outs):
            block = blocks[0]
            for i in range(1, n):
                block = jnp.where(lax.rem(me + s, n) == i, blocks[i], block)
            out[:, cs] = block
        return 0

    lax.fori_loop(0, width // nt, columns, 0)


def moments_kernel(n, m_ref, s_ref, *refs):
    parts, (moment_new, second_new, normed) = refs[:n], refs[n:]
    total = parts[0][...]
    for part in parts[1:]:
        total = total + part[...]
    moment_new[...], second_new[...], normed[...] = adam_moments(m_ref[...], s_ref[...], total)


def back_kernel(n, *refs):
    blocks, b_ref, keep, send, x_ref, o_ref = refs[:n], refs[n], *refs[n + 1 :]
    height, width = b_ref.shape
    rows = x_ref.shape[0]
    each = rows // n
    rt, jt = tile(height, 512), tile(width, 512)
    me = lax.axis_index("cols")
    for s, block in enumerate(blocks):
        x_ref[pl.ds(pl.multiple_of(lax.rem(me - s + n, n) * each, each), each), :] = block[...]

    def out_rows(r, _):
        rs = pl.ds(pl.multiple_of(r * rt, rt), rt)

        def inner(j, total):
            js = pl.ds(pl.multiple_of(j * jt, jt), jt)
            high, low = split(b_ref[rs, js])
            xh, xl = split(x_ref[:, js])
            first = lax.dot_general(jnp.concatenate([xh, xl]), high, TRANSPOSED, preferred_element_type=F32)
            second = lax.dot_general(xh, low, TRANSPOSED, preferred_element_type=F32)
            return total + first[:rows] + first[rows:] + second

        o_ref[:, rs] = lax.fori_loop(0, width // jt, inner, jnp.zeros((rows, rt), F32))
        return 0

    lax.fori_loop(0, height // rt, out_rows, 0)
    pairs, _, four, _ = keep.shape[0], 0, keep.shape[1], 0
    odd = lax.rem(lax.axis_index("rows"), 2) == 1
    whole = o_ref[...].reshape(pairs, 2, four, height)
    keep[...] = jnp.where(odd, whole[:, 1], whole[:, 0])
    send[...] = jnp.where(odd, whole[:, 0], whole[:, 1])


def fold_kernel(keep, got, *outs):
    chips = len(outs)
    chip = lax.axis_index("rows") // 2
    total = keep[...] + got[...]
    for s, out in enumerate(outs):
        block = total[0]
        for i in range(1, chips):
            block = jnp.where(lax.rem(chip + s, chips) == i, total[i], block)
        out[...] = block


def body(gradient, basis, moment, second):
    n, m = lax.axis_size("cols"), lax.axis_size("rows")
    each, width = moment.shape
    four, height = gradient.shape
    held = pltpu.with_memory_space_constraint(basis, pltpu.VMEM)
    gathered = lax.all_gather(gradient, "rows", axis=0)
    parts = call(rotate_kernel, [f32(each, width)] * n, gathered, held)

    def along(x, axis, size, s, step=1):
        pairs = [(i, (i // step + s) % (size // step) * step + i % step) for i in range(size)]
        return lax.ppermute(x, axis, pairs)

    parts = [parts[0]] + [along(parts[s], "cols", n, s) for s in range(1, n)]
    moment_new, second_new, normed = call(
        functools.partial(moments_kernel, n), [f32(each, width)] * 3, moment, second, *parts
    )
    blocks = [normed] + [along(normed, "cols", n, s) for s in range(1, n)]
    chips = m // 2
    keep, send = pl.pallas_call(
        functools.partial(back_kernel, n),
        out_shape=[f32(chips, four, height)] * 2,
        in_specs=[WHOLE] * (n + 1),
        out_specs=[WHOLE] * 2,
        scratch_shapes=[pltpu.VMEM((n * each, width), F32), pltpu.VMEM((m * four, height), F32)],
        compiler_params=pltpu.CompilerParams(vmem_limit_bytes=20 << 20),
    )(*blocks, held)
    got = lax.ppermute(send, "rows", [(i, i ^ 1) for i in range(m)])
    pieces = call(fold_kernel, [f32(four, height)] * chips, keep, got)
    update = pieces[0]
    for s in range(1, chips):
        update = update + along(pieces[s], "rows", m, s, 2)
    return (update, moment_new, second_new)


def solution(mesh):
    placed = (P("rows", "cols"), P("cols", "rows"), P("cols", "rows"), P("cols", "rows"))
    return jax.shard_map(
        body,
        mesh=mesh,
        in_specs=placed,
        out_specs=(P("rows", "cols"), P("cols", "rows"), P("cols", "rows")),
        check_vma=False,
    )
```

```python
import functools

import jax
import jax.numpy as jnp
from jax import lax
from jax.experimental import pallas as pl
from jax.experimental.pallas import tpu as pltpu
from jax.sharding import PartitionSpec as P

F32, BF16 = jnp.float32, jnp.bfloat16
WHOLE = pl.BlockSpec(memory_space=pltpu.VMEM)
FAR = pl.BlockSpec(memory_space=pltpu.HBM)
ANY = pl.BlockSpec(memory_space=pl.ANY)
TRANSPOSED = (((1,), (1,)), ((), ()))
MIB = 1 << 20
SHARES = (2, 1, 5)
BUFFERS = 3


def f32(*shape):
    return jax.ShapeDtypeStruct(shape, F32)


def cost(moved, flops=0):
    return pl.CostEstimate(flops=flops, bytes_accessed=moved, transcendentals=0)


def params(mib):
    return pltpu.CompilerParams(vmem_limit_bytes=mib * MIB)


def adam_moments(moment, second, rotated):
    moment_new = 0.9 * moment + 0.1 * rotated
    second_new = 0.95 * second + 0.05 * rotated * rotated
    normed = moment_new / (1.0 - 0.9**10) / (jnp.sqrt(second_new / (1.0 - 0.95**10)) + 1e-08)
    return (moment_new, second_new, normed)


def split(x):
    high = x.astype(BF16)
    return high, (x - high.astype(F32)).astype(BF16)


def load_kernel(first, count, after, *refs):
    b_ref, high_ref, low_ref, buf, sems = refs[after:]
    depth, rows, _ = buf.shape

    def copy(i):
        at = pl.ds(pl.multiple_of((first + i) * rows, rows), rows)
        return pltpu.make_async_copy(b_ref.at[at, :], buf.at[lax.rem(i, depth)], sems.at[lax.rem(i, depth)])

    for i in range(depth):
        copy(i).start()

    def step(i, _):
        copy(i).wait()
        at = pl.ds(pl.multiple_of(i * rows, rows), rows)
        high_ref[at, :], low_ref[at, :] = split(buf[lax.rem(i, depth)])

        @pl.when(i + depth < count)
        def _():
            copy(i + depth).start()

        return 0

    lax.fori_loop(0, count, step, 0)


def load(basis, first, count, tile, *after):
    width = basis.shape[1]
    depth = min(count, BUFFERS)
    return list(
        pl.pallas_call(
            functools.partial(load_kernel, first, count, len(after)),
            out_shape=[pltpu.VMEM((count * tile, width), BF16)] * 2,
            in_specs=[ANY] * len(after) + [FAR],
            out_specs=[WHOLE] * 2,
            scratch_shapes=[pltpu.VMEM((depth, tile, width), F32), pltpu.SemaphoreType.DMA((depth,))],
            cost_estimate=cost(count * tile * width * 8),
            compiler_params=params(8),
        )(*after, basis)
    )


def pack_kernel(*refs):
    _, *parts, out = refs
    for i, part in enumerate(parts):
        out[i] = part[...]


def rotate_kernel(n, kept, own_ref, got_ref, *refs):
    pieces, b_ref, (*outs, rest), (g_ref, total, sems) = (
        refs[:kept], refs[kept], refs[kept + 1 : kept + n + 2], refs[kept + n + 2 :]
    )
    steps, (depth, width) = sems.shape[0], rest.shape
    rows = depth // steps
    first = sum(high.shape[0] for high in pieces[::2])
    columns = min(width, 256)

    def copy(i):
        from_row, to_row = (pl.multiple_of(x, rows) for x in (first + i * rows, i * rows))
        return pltpu.make_async_copy(b_ref.at[pl.ds(from_row, rows), :], rest.at[pl.ds(to_row, rows), :], sems.at[i])

    for i in range(steps):
        copy(i).start()
    even = lax.rem(lax.axis_index("rows"), 2) == 0
    own, got = own_ref[...].astype(F32), got_ref[...].astype(F32)
    both = jnp.concatenate([jnp.where(even, own, got), jnp.where(even, got, own)], axis=1)
    g_ref[...] = both.reshape(g_ref.shape).astype(BF16)
    total[...] = jnp.zeros_like(total)

    def add(row, take):
        g = g_ref[:, pl.ds(pl.multiple_of(row, rows), rows)]
        for j in range(width // columns):
            at = slice(j * columns, (j + 1) * columns)
            high, low = take(at)
            total[:, at] += jnp.dot(g, high, preferred_element_type=F32) + jnp.dot(g, low, preferred_element_type=F32)

    done = 0
    for high, low in zip(pieces[::2], pieces[1::2]):

        def step(i, _, high=high, low=low, done=done):
            at = pl.ds(pl.multiple_of(i * rows, rows), rows)
            add(done + i * rows, lambda cs: (high[at, cs], low[at, cs]))
            return 0

        lax.fori_loop(0, high.shape[0] // rows, step, 0)
        done += high.shape[0]

    def step(i, _):
        copy(i).wait()
        at = pl.ds(pl.multiple_of(i * rows, rows), rows)
        add(first + i * rows, lambda cs: split(rest[at, cs]))
        return 0

    lax.fori_loop(0, steps, step, 0)
    chips, pair = own_ref.shape[0], 2 * own_ref.shape[1]
    chip = lax.axis_index("rows") // 2
    each = chips // n
    for s, out in enumerate(outs):
        place = (lax.axis_index("cols") ^ s) * each
        for i in range(each):
            slot = chip ^ (place + i)
            out[i * pair : (i + 1) * pair, :] = total[pl.ds(pl.multiple_of(slot * pair, pair), pair), :]


def moments_kernel(n, m_ref, s_ref, *refs):
    parts, (moment_new, second_new, normed) = refs[:n], refs[-3:]
    total = parts[0][...]
    for part in parts[1:]:
        total = total + part[...]
    moment_new[...], second_new[...], normed[...] = adam_moments(m_ref[...], s_ref[...], total)


def back_kernel(n, kept, *refs):
    blocks, pieces, (keep, send, x_ref, x2_ref, o_ref) = refs[:n], refs[n : n + kept], refs[n + kept :]
    each, rows = blocks[0].shape[0], x_ref.shape[0]
    for s, block in enumerate(blocks):
        place = (lax.axis_index("cols") ^ s) * each
        x_ref[pl.ds(pl.multiple_of(place, each), each), :] = block[...]
    high, low = split(x_ref[...])
    x2_ref[:rows, :], x2_ref[rows:, :] = high, low
    *pieces, rest = pieces
    done = 0

    def products(size, block, take):
        def step(i, _):
            high, low = take(pl.ds(pl.multiple_of(i * block, block), block))
            first = lax.dot_general(x2_ref[...], high, TRANSPOSED, preferred_element_type=F32)
            second = lax.dot_general(x2_ref[:rows, :], low, TRANSPOSED, preferred_element_type=F32)
            to = pl.ds(pl.multiple_of(done + i * block, 128), block)
            o_ref[:, to] = first[:rows] + first[rows:] + second
            return 0

        lax.fori_loop(0, size // block, step, 0)
        return size

    for high, low in zip(pieces[::2], pieces[1::2]):
        size = high.shape[0]
        done += products(size, min(size, 1024), lambda at: (high[at, :], low[at, :]))
    products(rest.shape[0], o_ref.shape[1] // 8, lambda at: split(rest[at, :]))
    odd = lax.rem(lax.axis_index("rows"), 2) == 1
    chips, four, height = keep.shape
    whole = o_ref[...].reshape(chips, 2, four, height)
    keep[...] = jnp.where(odd, whole[:, 1], whole[:, 0])
    send[...] = jnp.where(odd, whole[:, 0], whole[:, 1])


def fold_kernel(keep, got, *outs):
    chip = lax.axis_index("rows") // 2
    total = keep[...] + got[...]
    for s, out in enumerate(outs):
        block = total[0]
        for i in range(1, len(outs)):
            block = jnp.where((chip ^ s) == i, total[i], block)
        out[...] = block


def body(gradient, basis, moment, second):
    n, m = lax.axis_size("cols"), lax.axis_size("rows")
    chips = m // 2
    each, width = moment.shape
    four, height = gradient.shape
    tile = height // 16
    basis = pltpu.with_memory_space_constraint(basis, pltpu.HBM)

    def along_rows(x, s):
        return lax.ppermute(x, "rows", [(i, i ^ s) for i in range(m)])

    def along_cols(x, s):
        return lax.ppermute(x, "cols", [(i, i ^ s) for i in range(n)])

    from_chips = [gradient] + [along_rows(gradient, 2 * s) for s in range(1, chips)]
    pieces = load(basis, 0, 2 * SHARES[0], tile)
    own = pl.pallas_call(
        pack_kernel,
        out_shape=jax.ShapeDtypeStruct((chips, four, height), BF16),
        in_specs=[ANY] + [WHOLE] * chips,
        out_specs=WHOLE,
        compiler_params=params(4),
    )(pieces[0], *from_chips)
    got = along_rows(own, 1)
    pieces = pieces + load(basis, 2 * SHARES[0], 2 * SHARES[1], tile, own)
    *parts, rest = pl.pallas_call(
        functools.partial(rotate_kernel, n, len(pieces)),
        out_shape=[f32(each, width)] * n + [pltpu.VMEM((SHARES[2] * height // 8, width), F32)],
        in_specs=[WHOLE] * (len(pieces) + 2) + [FAR],
        out_specs=[WHOLE] * (n + 1),
        scratch_shapes=[
            pltpu.VMEM((n * each, height), BF16),
            pltpu.VMEM((n * each, width), F32),
            pltpu.SemaphoreType.DMA((SHARES[2],)),
        ],
        cost_estimate=cost(height * width * 4),
        compiler_params=params(8),
    )(own, got, *pieces, basis)
    pieces = [pltpu.with_memory_space_constraint(x, pltpu.VMEM) for x in pieces + [rest]]
    parts = [parts[0]] + [along_cols(parts[s], s) for s in range(1, n)]
    moment_new, second_new, normed = pl.pallas_call(
        functools.partial(moments_kernel, n),
        out_shape=[f32(each, width)] * 3,
        in_specs=[WHOLE] * (n + 2) + [WHOLE] * len(pieces),
        out_specs=[WHOLE] * 3,
        compiler_params=params(4),
    )(moment, second, *parts, *pieces)
    blocks = [normed] + [along_cols(normed, s) for s in range(1, n)]
    keep, send = pl.pallas_call(
        functools.partial(back_kernel, n, len(pieces)),
        out_shape=[f32(chips, four, height)] * 2,
        in_specs=[WHOLE] * (n + len(pieces)),
        out_specs=[WHOLE] * 2,
        scratch_shapes=[
            pltpu.VMEM((n * each, width), F32),
            pltpu.VMEM((2 * n * each, width), BF16),
            pltpu.VMEM((n * each, height), F32),
        ],
        cost_estimate=cost(height * width * 4),
        compiler_params=params(8),
    )(*blocks, *pieces)
    got = along_rows(send, 1)
    pieces = pl.pallas_call(
        fold_kernel,
        out_shape=[f32(four, height)] * chips,
        in_specs=[WHOLE] * 2,
        out_specs=[WHOLE] * chips,
        compiler_params=params(8),
    )(keep, got)
    update = pieces[0]
    for s in range(1, chips):
        update = update + along_rows(pieces[s], 2 * s)
    return (update, moment_new, second_new)


def solution(mesh):
    placed = (P("rows", "cols"), P("cols", "rows"), P("cols", "rows"), P("cols", "rows"))
    return jax.shard_map(
        body,
        mesh=mesh,
        in_specs=placed,
        out_specs=(P("rows", "cols"), P("cols", "rows"), P("cols", "rows")),
        check_vma=False,
    )
```

```python
import functools

import jax
import jax.numpy as jnp
from jax import lax
from jax.experimental import pallas as pl
from jax.experimental.pallas import tpu as pltpu
from jax.sharding import PartitionSpec as P

F32, BF16 = jnp.float32, jnp.bfloat16
WHOLE = pl.BlockSpec(memory_space=pltpu.VMEM)
FAR = pl.BlockSpec(memory_space=pltpu.HBM)
ANY = pl.BlockSpec(memory_space=pl.ANY)
TRANSPOSED = (((1,), (1,)), ((), ()))
LIMIT = 6 << 20
PARTS = 4


def f32(*shape):
    return jax.ShapeDtypeStruct(shape, F32)


def turned(rows, width):
    return [pltpu.VMEM((width, rows), BF16)] * 2


def kernel(body, outs, ins, args, scratch=(), moved=0):
    return pl.pallas_call(
        body,
        out_shape=outs,
        in_specs=ins,
        out_specs=jax.tree.map(lambda _: WHOLE, outs),
        scratch_shapes=scratch,
        cost_estimate=pl.CostEstimate(flops=0, bytes_accessed=moved, transcendentals=0) if moved else None,
        compiler_params=pltpu.CompilerParams(vmem_limit_bytes=LIMIT),
    )(*args)


def span(i, size):
    return pl.ds(pl.multiple_of(i * size, size), size)


def adam_moments(moment, second, rotated):
    moment_new = 0.9 * moment + 0.1 * rotated
    second_new = 0.95 * second + 0.05 * rotated * rotated
    normed = moment_new / (1.0 - 0.9**10) / (jnp.sqrt(second_new / (1.0 - 0.95**10)) + 1e-08)
    return (moment_new, second_new, normed)


def split(x):
    high = x.astype(BF16)
    return high, (x - high.astype(F32)).astype(BF16)


def stage_kernel(far, near, sem):
    copy = pltpu.make_async_copy(far, near, sem)
    copy.start()
    copy.wait()


def pack_kernel(own, got, out):
    even = lax.rem(lax.axis_index("rows"), 2) == 0
    own, got = own[...].astype(F32), got[...].astype(F32)
    out[...] = jnp.concatenate([jnp.where(even, own, got), jnp.where(even, got, own)], axis=0).astype(BF16)


def turn(take, high_ref, low_ref, row, rows):
    width = high_ref.shape[0]
    columns = min(width, 512)
    for j in range(width // columns):
        at = slice(j * columns, (j + 1) * columns)
        high, low = split(take(at))
        high_ref[at, pl.ds(row, rows)], low_ref[at, pl.ds(row, rows)] = high.T, low.T


def load_kernel(_, b_ref, near, sems):
    count = sems.shape[0]
    rows = near.shape[0] // count
    copies = [
        pltpu.make_async_copy(b_ref.at[pl.ds(i * rows, rows), :], near.at[pl.ds(i * rows, rows), :], sems.at[i])
        for i in range(count)
    ]
    for copy in copies:
        copy.start()
    for copy in copies:
        copy.wait()


def turn_kernel(b_ref, *refs):
    high_ref, low_ref = refs[-2:]
    rows = min(b_ref.shape[0], 512)
    for i in range(b_ref.shape[0] // rows):
        turn(lambda at, i=i: b_ref[i * rows : (i + 1) * rows, at], high_ref, low_ref, i * rows, rows)


def rotate_kernel(n, chips, *refs):
    blocks, (ready, b_ref), refs = refs[:chips], refs[chips : chips + 2], refs[chips + 2 :]
    outs, parts, (g_ref, total, sems) = refs[:n], refs[n : n + PARTS - 1], refs[n + PARTS - 1 :]
    part, width = parts[0].shape
    rows, columns = min(part, 256), min(width, 256)
    tiles = [(p, i) for p in range(PARTS - 1) for i in range(part // rows)]

    def copy(k):
        p, i = tiles[k]
        return pltpu.make_async_copy(
            b_ref.at[pl.ds((p + 1) * part + i * rows, rows), :], parts[p].at[pl.ds(i * rows, rows), :], sems.at[k]
        )

    def copy_at(p, i):
        return pltpu.make_async_copy(
            b_ref.at[span((p + 1) * (part // rows) + i, rows), :],
            parts[p].at[span(i, rows), :],
            sems.at[p * (part // rows) + i],
        )

    for k in range(len(tiles)):
        copy(k).start()
    g_ref[...] = jnp.concatenate([block[...].astype(F32) for block in blocks], axis=0).astype(BF16)
    total[...] = jnp.zeros_like(total)
    for p, ref in enumerate((ready, *parts)):

        def tile(i, _, p=p, ref=ref):
            if p:
                copy_at(p - 1, i).wait()
            g = g_ref[:, pl.ds(pl.multiple_of(p * part + i * rows, rows), rows)]
            for j in range(width // columns):
                at = slice(j * columns, (j + 1) * columns)
                high, low = split(ref[span(i, rows), at])
                total[:, at] += jnp.dot(g, high, preferred_element_type=F32) + jnp.dot(
                    g, low, preferred_element_type=F32
                )
            return 0

        lax.fori_loop(0, part // rows, tile, 0)
    pair = blocks[0].shape[0]
    chip = lax.axis_index("rows") // 2
    each = chips // n
    for s, out in enumerate(outs):
        place = (lax.axis_index("cols") ^ s) * each
        for i in range(each):
            out[i * pair : (i + 1) * pair, :] = total[span(chip ^ (place + i), pair), :]


def normed_kernel(n, m_ref, s_ref, *refs):
    parts, (normed, rotated) = refs[:n], refs[-2:]
    total = parts[0][...]
    for part in parts[1:]:
        total = total + part[...]
    rotated[...] = total
    normed[...] = adam_moments(m_ref[...], s_ref[...], total)[2]


def moments_kernel(m_ref, s_ref, rotated, moment_new, second_new):
    moment_new[...], second_new[...], _ = adam_moments(m_ref[...], s_ref[...], rotated[...])


def back_kernel(n, kept, *refs):
    blocks, pieces, rest = refs[:n], refs[n : n + kept], refs[n + kept : -5]
    keep, send, x_ref, x2_ref, o_ref = refs[-5:]
    each, rows = blocks[0].shape[0], x_ref.shape[0]
    for s, block in enumerate(blocks):
        x_ref[span(lax.axis_index("cols") ^ s, each), :] = block[...]
    high, low = split(x_ref[...])
    x2_ref[:rows, :], x2_ref[rows:, :] = high, low
    part = rest[0].shape[0]
    size = min(part, 512)

    def store(to, first, second):
        o_ref[:, to : to + size] = first[:rows] + first[rows:] + second

    for p, (high, low) in enumerate(zip(pieces[::2], pieces[1::2])):
        for i in range(part // size):
            at = slice(i * size, (i + 1) * size)
            first = jnp.dot(x2_ref[...], high[:, at], preferred_element_type=F32)
            second = jnp.dot(x2_ref[:rows, :], low[:, at], preferred_element_type=F32)
            store(p * part + i * size, first, second)
    for p, ref in enumerate(rest):
        for i in range(part // size):
            high, low = split(ref[i * size : (i + 1) * size, :])
            first = lax.dot_general(x2_ref[...], high, TRANSPOSED, preferred_element_type=F32)
            second = lax.dot_general(x2_ref[:rows, :], low, TRANSPOSED, preferred_element_type=F32)
            store((len(pieces) // 2 + p) * part + i * size, first, second)
    odd = lax.rem(lax.axis_index("rows"), 2) == 1
    chips, four, height = keep.shape
    whole = o_ref[...].reshape(chips, 2, four, height)
    keep[...] = jnp.where(odd, whole[:, 1], whole[:, 0])
    send[...] = jnp.where(odd, whole[:, 0], whole[:, 1])


def fold_kernel(keep, got, *outs):
    chip = lax.axis_index("rows") // 2
    total = keep[...] + got[...]
    for s, out in enumerate(outs):
        block = total[0]
        for i in range(1, len(outs)):
            block = jnp.where((chip ^ s) == i, total[i], block)
        out[...] = block


def step_on_device(gradient, basis, moment, second):
    n, m = lax.axis_size("cols"), lax.axis_size("rows")
    chips = m // 2
    each, width = moment.shape
    four, height = gradient.shape
    part = height // PARTS
    partbytes = part * width * 4

    def along(x, axis, size, s):
        return lax.ppermute(x, axis, [(i, i ^ s) for i in range(size)])

    def along_rows(x, s):
        return along(x, "rows", m, s)

    def along_cols(x, s):
        return along(x, "cols", n, s)

    basis = pltpu.with_memory_space_constraint(basis, pltpu.HBM)
    partner = along_rows(gradient, 1)
    own = kernel(
        stage_kernel,
        pltpu.VMEM(gradient.shape, BF16),
        [FAR],
        (pltpu.with_memory_space_constraint(gradient, pltpu.HBM),),
        [pltpu.SemaphoreType.DMA],
        four * height * 4,
    )
    own = kernel(pack_kernel, jax.ShapeDtypeStruct((2 * four, height), BF16), [WHOLE] * 2, (own, partner))
    from_chips = [own] + [along_rows(own, 2 * s) for s in range(1, chips)]
    first = kernel(
        load_kernel,
        pltpu.VMEM((part, width), F32),
        [ANY, FAR],
        (own, basis),
        [pltpu.SemaphoreType.DMA((4,))],
        2 * partbytes,
    )
    results = kernel(
        functools.partial(rotate_kernel, n, chips),
        [f32(each, width)] * n + [pltpu.VMEM((part, width), F32)] * (PARTS - 1),
        [WHOLE] * (chips + 1) + [FAR],
        (*from_chips, first, basis),
        [
            pltpu.VMEM((n * each, height), BF16),
            pltpu.VMEM((n * each, width), F32),
            pltpu.SemaphoreType.DMA((height // min(part, 256),)),
        ],
        PARTS * partbytes,
    )
    parts, (early, later, *rest) = results[:n], [
        pltpu.with_memory_space_constraint(x, pltpu.VMEM) for x in (first, *results[n:])
    ]
    parts = [parts[0]] + [along_cols(parts[s], s) for s in range(1, n)]
    pieces = list(
        kernel(turn_kernel, turned(part, width), [WHOLE] * (2 + len(rest)), (early, later, *rest), (), 2 * partbytes)
    )
    pieces = [pltpu.with_memory_space_constraint(x, pltpu.VMEM) for x in pieces]
    normed, rotated = kernel(
        functools.partial(normed_kernel, n),
        [f32(each, width)] * 2,
        [WHOLE] * (n + 3 + len(pieces) + len(rest)),
        (moment, second, *parts, *pieces, later, *rest),
    )
    moment_new, second_new = kernel(
        moments_kernel, [f32(each, width)] * 2, [WHOLE] * 3, (moment, second, rotated), (), 8 * each * width * 4
    )
    blocks = [normed] + [along_cols(normed, s) for s in range(1, n)]
    pieces += list(kernel(turn_kernel, turned(part, width), [WHOLE] * (1 + len(rest)), (later, *rest), (), 2 * partbytes))
    keep, send = kernel(
        functools.partial(back_kernel, n, len(pieces)),
        [f32(chips, four, height)] * 2,
        [WHOLE] * (n + len(pieces) + len(rest)),
        (*blocks, *pieces, *rest),
        [
            pltpu.VMEM((n * each, width), F32),
            pltpu.VMEM((2 * n * each, width), BF16),
            pltpu.VMEM((n * each, height), F32),
        ],
        PARTS * partbytes,
    )
    got = along_rows(send, 1)
    halves = kernel(fold_kernel, [f32(four, height)] * chips, [WHOLE] * 2, (keep, got))
    update = halves[0]
    for s in range(1, chips):
        update = update + along_rows(halves[s], 2 * s)
    return (update, moment_new, second_new)


def solution(mesh):
    placed = (P("rows", "cols"), P("cols", "rows"), P("cols", "rows"), P("cols", "rows"))
    return jax.shard_map(
        step_on_device,
        mesh=mesh,
        in_specs=placed,
        out_specs=(P("rows", "cols"), P("cols", "rows"), P("cols", "rows")),
        check_vma=False,
    )
```

```python
import functools

import jax
import jax.numpy as jnp
from jax import lax
from jax.experimental import pallas as pl
from jax.experimental.pallas import tpu as pltpu
from jax.sharding import PartitionSpec as P

F32, BF16 = jnp.float32, jnp.bfloat16
WHOLE = pl.BlockSpec(memory_space=pltpu.VMEM)
FAR = pl.BlockSpec(memory_space=pltpu.HBM)
ANY = pl.BlockSpec(memory_space=pl.ANY)
TRANSPOSED = (((1,), (1,)), ((), ()))
LIMIT = 6 << 20
PARTS = (5, 5, 3, 3)


def f32(*shape):
    return jax.ShapeDtypeStruct(shape, F32)


def turned(rows, width):
    return [pltpu.VMEM((width, rows), BF16)] * 2


def kernel(body, outs, ins, args, scratch=(), moved=0):
    return pl.pallas_call(
        body,
        out_shape=outs,
        in_specs=ins,
        out_specs=jax.tree.map(lambda _: WHOLE, outs),
        scratch_shapes=scratch,
        cost_estimate=pl.CostEstimate(flops=0, bytes_accessed=moved, transcendentals=0) if moved else None,
        compiler_params=pltpu.CompilerParams(vmem_limit_bytes=LIMIT),
    )(*args)


def span(i, size):
    return pl.ds(pl.multiple_of(i * size, size), size)


def adam_moments(moment, second, rotated):
    moment_new = 0.9 * moment + 0.1 * rotated
    second_new = 0.95 * second + 0.05 * rotated * rotated
    normed = moment_new / (1.0 - 0.9**10) / (jnp.sqrt(second_new / (1.0 - 0.95**10)) + 1e-08)
    return (moment_new, second_new, normed)


def split(x):
    high = x.astype(BF16)
    return high, (x - high.astype(F32)).astype(BF16)


def stage_kernel(far, near, sem):
    copy = pltpu.make_async_copy(far, near, sem)
    copy.start()
    copy.wait()


def pack_kernel(own, got, out):
    even = lax.rem(lax.axis_index("rows"), 2) == 0
    own, got = own[...].astype(F32), got[...].astype(F32)
    out[...] = jnp.concatenate([jnp.where(even, own, got), jnp.where(even, got, own)], axis=0).astype(BF16)


def turn(take, high_ref, low_ref, row, rows):
    width = high_ref.shape[0]
    columns = min(width, 512)
    for j in range(width // columns):
        at = slice(j * columns, (j + 1) * columns)
        high, low = split(take(at))
        high_ref[at, pl.ds(row, rows)], low_ref[at, pl.ds(row, rows)] = high.T, low.T


def load_kernel(_, b_ref, near, sems):
    count = sems.shape[0]
    rows = near.shape[0] // count
    copies = [
        pltpu.make_async_copy(b_ref.at[pl.ds(i * rows, rows), :], near.at[pl.ds(i * rows, rows), :], sems.at[i])
        for i in range(count)
    ]
    for copy in copies:
        copy.start()
    for copy in copies:
        copy.wait()


def turn_kernel(b_ref, *refs):
    high_ref, low_ref = refs[-2:]
    rows = min(b_ref.shape[0], 256)
    for i in range(b_ref.shape[0] // rows):
        turn(lambda at, i=i: b_ref[i * rows : (i + 1) * rows, at], high_ref, low_ref, i * rows, rows)


def rotate_kernel(n, chips, *refs):
    blocks, (ready, b_ref), refs = refs[:chips], refs[chips : chips + 2], refs[chips + 2 :]
    outs, parts, (g_ref, total, sems) = refs[:n], refs[n : n + len(PARTS) - 1], refs[n + len(PARTS) - 1 :]
    width = ready.shape[1]
    rows, columns = b_ref.shape[0] // 16, min(width, 256)
    begins = [sum(PARTS[:p]) for p in range(len(PARTS))]

    def copy(p, i):
        k = begins[p] + i
        return pltpu.make_async_copy(b_ref.at[span(k, rows), :], parts[p - 1].at[span(i, rows), :], sems.at[k])

    for p in range(1, len(PARTS)):
        for i in range(PARTS[p]):
            copy(p, i).start()
    g_ref[...] = jnp.concatenate([block[...].astype(F32) for block in blocks], axis=0).astype(BF16)
    total[...] = jnp.zeros_like(total)
    for p, ref in enumerate((ready, *parts)):

        def tile(i, _, p=p, ref=ref):
            if p:
                copy(p, i).wait()
            g = g_ref[:, span(begins[p] + i, rows)]
            for j in range(width // columns):
                at = slice(j * columns, (j + 1) * columns)
                high, low = split(ref[span(i, rows), at])
                total[:, at] += jnp.dot(g, high, preferred_element_type=F32) + jnp.dot(
                    g, low, preferred_element_type=F32
                )
            return 0

        lax.fori_loop(0, PARTS[p], tile, 0)
    pair = blocks[0].shape[0]
    chip = lax.axis_index("rows") // 2
    each = chips // n
    for s, out in enumerate(outs):
        place = (lax.axis_index("cols") ^ s) * each
        for i in range(each):
            out[i * pair : (i + 1) * pair, :] = total[span(chip ^ (place + i), pair), :]


def normed_kernel(n, m_ref, s_ref, *refs):
    parts, (normed, rotated) = refs[:n], refs[-2:]
    total = parts[0][...]
    for part in parts[1:]:
        total = total + part[...]
    rotated[...] = total
    normed[...] = adam_moments(m_ref[...], s_ref[...], total)[2]


def moments_kernel(m_ref, s_ref, rotated, moment_new, second_new):
    moment_new[...], second_new[...], _ = adam_moments(m_ref[...], s_ref[...], rotated[...])


def back_kernel(n, kept, *refs):
    blocks, pieces, rest = refs[:n], refs[n : n + kept], refs[n + kept : -5]
    keep, send, x_ref, x2_ref, o_ref = refs[-5:]
    each, rows = blocks[0].shape[0], x_ref.shape[0]
    for s, block in enumerate(blocks):
        x_ref[span(lax.axis_index("cols") ^ s, each), :] = block[...]
    high, low = split(x_ref[...])
    x2_ref[:rows, :], x2_ref[rows:, :] = high, low
    begins = [sum(PARTS[:p]) * o_ref.shape[1] // 16 for p in range(len(PARTS) + 1)]

    def store(p, first, second):
        o_ref[:, begins[p] : begins[p + 1]] = first[:rows] + first[rows:] + second

    for p, (high, low) in enumerate(zip(pieces[::2], pieces[1::2])):
        first = jnp.dot(x2_ref[...], high[...], preferred_element_type=F32)
        store(p, first, jnp.dot(x2_ref[:rows, :], low[...], preferred_element_type=F32))
    for p, ref in enumerate(rest, len(pieces) // 2):
        high, low = split(ref[...])
        first = lax.dot_general(x2_ref[...], high, TRANSPOSED, preferred_element_type=F32)
        store(p, first, lax.dot_general(x2_ref[:rows, :], low, TRANSPOSED, preferred_element_type=F32))
    odd = lax.rem(lax.axis_index("rows"), 2) == 1
    chips, four, height = keep.shape
    whole = o_ref[...].reshape(chips, 2, four, height)
    keep[...] = jnp.where(odd, whole[:, 1], whole[:, 0])
    send[...] = jnp.where(odd, whole[:, 0], whole[:, 1])


def fold_kernel(keep, got, *outs):
    chip = lax.axis_index("rows") // 2
    total = keep[...] + got[...]
    for s, out in enumerate(outs):
        block = total[0]
        for i in range(1, len(outs)):
            block = jnp.where((chip ^ s) == i, total[i], block)
        out[...] = block


def step_on_device(gradient, basis, moment, second):
    n, m = lax.axis_size("cols"), lax.axis_size("rows")
    chips = m // 2
    each, width = moment.shape
    four, height = gradient.shape
    sizes = [share * height // 16 for share in PARTS]
    moved = height * width * 4

    def along(x, axis, size, s):
        return lax.ppermute(x, axis, [(i, i ^ s) for i in range(size)])

    def along_rows(x, s):
        return along(x, "rows", m, s)

    def along_cols(x, s):
        return along(x, "cols", n, s)

    basis = pltpu.with_memory_space_constraint(basis, pltpu.HBM)
    partner = along_rows(gradient, 1)
    own = kernel(
        stage_kernel,
        pltpu.VMEM(gradient.shape, BF16),
        [FAR],
        (pltpu.with_memory_space_constraint(gradient, pltpu.HBM),),
        [pltpu.SemaphoreType.DMA],
        four * height * 4,
    )
    own = kernel(pack_kernel, jax.ShapeDtypeStruct((2 * four, height), BF16), [WHOLE] * 2, (own, partner))
    from_chips = [own] + [along_rows(own, 2 * s) for s in range(1, chips)]
    first = kernel(
        load_kernel,
        pltpu.VMEM((sizes[0], width), F32),
        [ANY, FAR],
        (own, basis),
        [pltpu.SemaphoreType.DMA((4,))],
        moved // 2,
    )
    results = kernel(
        functools.partial(rotate_kernel, n, chips),
        [f32(each, width)] * n + [pltpu.VMEM((size, width), F32) for size in sizes[1:]],
        [WHOLE] * (chips + 1) + [FAR],
        (*from_chips, first, basis),
        [
            pltpu.VMEM((n * each, height), BF16),
            pltpu.VMEM((n * each, width), F32),
            pltpu.SemaphoreType.DMA((16,)),
        ],
        moved,
    )
    parts, (early, later, *rest) = results[:n], [
        pltpu.with_memory_space_constraint(x, pltpu.VMEM) for x in (first, *results[n:])
    ]
    parts = [parts[0]] + [along_cols(parts[s], s) for s in range(1, n)]
    pieces = list(
        kernel(turn_kernel, turned(sizes[0], width), [WHOLE] * (2 + len(rest)), (early, later, *rest), (), moved // 2)
    )
    pieces = [pltpu.with_memory_space_constraint(x, pltpu.VMEM) for x in pieces]
    normed, rotated = kernel(
        functools.partial(normed_kernel, n),
        [f32(each, width)] * 2,
        [WHOLE] * (n + 3 + len(pieces) + len(rest)),
        (moment, second, *parts, *pieces, later, *rest),
    )
    moment_new, second_new = kernel(
        moments_kernel, [f32(each, width)] * 2, [WHOLE] * 3, (moment, second, rotated), (), 8 * each * width * 4
    )
    blocks = [normed] + [along_cols(normed, s) for s in range(1, n)]
    pieces += list(kernel(turn_kernel, turned(sizes[1], width), [WHOLE] * (1 + len(rest)), (later, *rest), (), moved // 2))
    keep, send = kernel(
        functools.partial(back_kernel, n, len(pieces)),
        [f32(chips, four, height)] * 2,
        [WHOLE] * (n + len(pieces) + len(rest)),
        (*blocks, *pieces, *rest),
        [
            pltpu.VMEM((n * each, width), F32),
            pltpu.VMEM((2 * n * each, width), BF16),
            pltpu.VMEM((n * each, height), F32),
        ],
        moved,
    )
    got = along_rows(send, 1)
    halves = kernel(fold_kernel, [f32(four, height)] * chips, [WHOLE] * 2, (keep, got))
    update = halves[0]
    for s in range(1, chips):
        update = update + along_rows(halves[s], 2 * s)
    return (update, moment_new, second_new)


def solution(mesh):
    placed = (P("rows", "cols"), P("cols", "rows"), P("cols", "rows"), P("cols", "rows"))
    return jax.shard_map(
        step_on_device,
        mesh=mesh,
        in_specs=placed,
        out_specs=(P("rows", "cols"), P("cols", "rows"), P("cols", "rows")),
        check_vma=False,
    )
```

```python
import functools

import jax
import jax.numpy as jnp
from jax import lax
from jax.experimental import pallas as pl
from jax.experimental.pallas import tpu as pltpu
from jax.sharding import PartitionSpec as P

F32, BF16 = jnp.float32, jnp.bfloat16
WHOLE = pl.BlockSpec(memory_space=pltpu.VMEM)
FAR = pl.BlockSpec(memory_space=pltpu.HBM)
ANY = pl.BlockSpec(memory_space=pl.ANY)
LIMIT = 6 << 20
PARTS = (5, 5, 3, 3)


def f32(*shape):
    return jax.ShapeDtypeStruct(shape, F32)


def turned(rows, width):
    return [pltpu.VMEM((width, rows), BF16)] * 2


def kernel(body, outs, ins, args, scratch=(), moved=0):
    return pl.pallas_call(
        body,
        out_shape=outs,
        in_specs=ins,
        out_specs=jax.tree.map(lambda _: WHOLE, outs),
        scratch_shapes=scratch,
        cost_estimate=pl.CostEstimate(flops=0, bytes_accessed=moved, transcendentals=0) if moved else None,
        compiler_params=pltpu.CompilerParams(vmem_limit_bytes=LIMIT),
    )(*args)


def span(i, size):
    return pl.ds(pl.multiple_of(i * size, size), size)


def adam_moments(moment, second, rotated):
    moment_new = 0.9 * moment + 0.1 * rotated
    second_new = 0.95 * second + 0.05 * rotated * rotated
    normed = moment_new / (1.0 - 0.9**10) / (jnp.sqrt(second_new / (1.0 - 0.95**10)) + 1e-08)
    return (moment_new, second_new, normed)


def split(x):
    high = x.astype(BF16)
    return high, (x - high.astype(F32)).astype(BF16)


def stage_kernel(far, near, sem):
    copy = pltpu.make_async_copy(far, near, sem)
    copy.start()
    copy.wait()


def pack_kernel(own, got, out):
    even = lax.rem(lax.axis_index("rows"), 2) == 0
    own, got = own[...].astype(F32), got[...].astype(F32)
    out[...] = jnp.concatenate([jnp.where(even, own, got), jnp.where(even, got, own)], axis=0).astype(BF16)


def turn(take, high_ref, low_ref, row, rows):
    width = high_ref.shape[0]
    columns = min(width, 512)
    for j in range(width // columns):
        at = slice(j * columns, (j + 1) * columns)
        high, low = split(take(at))
        high_ref[at, pl.ds(row, rows)], low_ref[at, pl.ds(row, rows)] = high.T, low.T


def load_kernel(_, b_ref, near, sems):
    count = sems.shape[0]
    rows = near.shape[0] // count
    copies = [
        pltpu.make_async_copy(b_ref.at[pl.ds(i * rows, rows), :], near.at[pl.ds(i * rows, rows), :], sems.at[i])
        for i in range(count)
    ]
    for copy in copies:
        copy.start()
    for copy in copies:
        copy.wait()


def turn_kernel(b_ref, *refs):
    high_ref, low_ref = refs[-2:]
    rows = min(b_ref.shape[0], 256)
    for i in range(b_ref.shape[0] // rows):
        turn(lambda at, i=i: b_ref[i * rows : (i + 1) * rows, at], high_ref, low_ref, i * rows, rows)


def rotate_kernel(n, chips, *refs):
    blocks, (ready, b_ref), refs = refs[:chips], refs[chips : chips + 2], refs[chips + 2 :]
    outs, parts, (g_ref, total, sems) = refs[:n], refs[n : n + len(PARTS) - 1], refs[n + len(PARTS) - 1 :]
    width = ready.shape[1]
    rows, columns = b_ref.shape[0] // 16, min(width, 256)
    begins = [sum(PARTS[:p]) for p in range(len(PARTS))]

    def copy(p, i):
        k = begins[p] + i
        return pltpu.make_async_copy(b_ref.at[span(k, rows), :], parts[p - 1].at[span(i, rows), :], sems.at[k])

    for p in range(1, len(PARTS)):
        for i in range(PARTS[p]):
            copy(p, i).start()
    g_ref[...] = jnp.concatenate([block[...].astype(F32) for block in blocks], axis=0).astype(BF16)
    total[...] = jnp.zeros_like(total)
    for p, ref in enumerate((ready, *parts)):

        def tile(i, _, p=p, ref=ref):
            if p:
                copy(p, i).wait()
            g = g_ref[:, span(begins[p] + i, rows)]
            for j in range(width // columns):
                at = slice(j * columns, (j + 1) * columns)
                high, low = split(ref[span(i, rows), at])
                total[:, at] += jnp.dot(g, high, preferred_element_type=F32) + jnp.dot(
                    g, low, preferred_element_type=F32
                )
            return 0

        lax.fori_loop(0, PARTS[p], tile, 0)
    pair = blocks[0].shape[0]
    chip = lax.axis_index("rows") // 2
    each = chips // n
    for s, out in enumerate(outs):
        place = (lax.axis_index("cols") ^ s) * each
        for i in range(each):
            out[i * pair : (i + 1) * pair, :] = total[span(chip ^ (place + i), pair), :]


def normed_kernel(n, m_ref, s_ref, *refs):
    parts, (normed, rotated) = refs[:n], refs[-2:]
    total = parts[0][...]
    for part in parts[1:]:
        total = total + part[...]
    rotated[...] = total
    normed[...] = adam_moments(m_ref[...], s_ref[...], total)[2]


def moments_kernel(m_ref, s_ref, rotated, moment_new, second_new):
    moment_new[...], second_new[...], _ = adam_moments(m_ref[...], s_ref[...], rotated[...])


def back_kernel(n, kept, *refs):
    blocks, pieces, rest = refs[:n], refs[n : n + kept], refs[n + kept : -7]
    keep, send, x_ref, x2_ref, o_ref, turned_high, turned_low = refs[-7:]
    each, rows = blocks[0].shape[0], x_ref.shape[0]
    for s, block in enumerate(blocks):
        x_ref[span(lax.axis_index("cols") ^ s, each), :] = block[...]
    high, low = split(x_ref[...])
    x2_ref[:rows, :], x2_ref[rows:, :] = high, low
    begins = [sum(PARTS[:p]) * o_ref.shape[1] // 16 for p in range(len(PARTS) + 1)]

    size = o_ref.shape[1] // 16

    def multiply(to, high, low):
        first = jnp.dot(x2_ref[...], high, preferred_element_type=F32)
        second = jnp.dot(x2_ref[:rows, :], low, preferred_element_type=F32)
        o_ref[:, to : to + size] = first[:rows] + first[rows:] + second

    ready = [
        (begins[p] + i * size, high, low, i)
        for p, (high, low) in enumerate(zip(pieces[::2], pieces[1::2]))
        for i in range(PARTS[p])
    ]
    waiting = [
        (begins[p] + i * size, ref, i) for p, ref in enumerate(rest, len(pieces) // 2) for i in range(PARTS[p])
    ]
    slots = turned_high.shape[0]
    for k, (_, ref, i) in enumerate(waiting):
        turn(lambda at, ref=ref, i=i: ref[i * size : (i + 1) * size, at], turned_high.at[k % slots], turned_low.at[k % slots], 0, size)
        for to, high, low, j in ready[k * len(ready) // len(waiting) : (k + 1) * len(ready) // len(waiting)]:
            multiply(to, high[:, j * size : (j + 1) * size], low[:, j * size : (j + 1) * size])
        if k:
            multiply(waiting[k - 1][0], turned_high[(k - 1) % slots], turned_low[(k - 1) % slots])
    multiply(waiting[-1][0], turned_high[(len(waiting) - 1) % slots], turned_low[(len(waiting) - 1) % slots])
    odd = lax.rem(lax.axis_index("rows"), 2) == 1
    chips, four, height = keep.shape
    whole = o_ref[...].reshape(chips, 2, four, height)
    keep[...] = jnp.where(odd, whole[:, 1], whole[:, 0])
    send[...] = jnp.where(odd, whole[:, 0], whole[:, 1])


def fold_kernel(keep, got, *outs):
    chip = lax.axis_index("rows") // 2
    total = keep[...] + got[...]
    for s, out in enumerate(outs):
        block = total[0]
        for i in range(1, len(outs)):
            block = jnp.where((chip ^ s) == i, total[i], block)
        out[...] = block


def step_on_device(gradient, basis, moment, second):
    n, m = lax.axis_size("cols"), lax.axis_size("rows")
    chips = m // 2
    each, width = moment.shape
    four, height = gradient.shape
    sizes = [share * height // 16 for share in PARTS]
    moved = height * width * 4

    def along(x, axis, size, s):
        return lax.ppermute(x, axis, [(i, i ^ s) for i in range(size)])

    def along_rows(x, s):
        return along(x, "rows", m, s)

    def along_cols(x, s):
        return along(x, "cols", n, s)

    basis = pltpu.with_memory_space_constraint(basis, pltpu.HBM)
    partner = along_rows(gradient, 1)
    own = kernel(
        stage_kernel,
        pltpu.VMEM(gradient.shape, BF16),
        [FAR],
        (pltpu.with_memory_space_constraint(gradient, pltpu.HBM),),
        [pltpu.SemaphoreType.DMA],
        four * height * 4,
    )
    own = kernel(pack_kernel, jax.ShapeDtypeStruct((2 * four, height), BF16), [WHOLE] * 2, (own, partner))
    from_chips = [own] + [along_rows(own, 2 * s) for s in range(1, chips)]
    first = kernel(
        load_kernel,
        pltpu.VMEM((sizes[0], width), F32),
        [ANY, FAR],
        (own, basis),
        [pltpu.SemaphoreType.DMA((4,))],
        moved // 2,
    )
    results = kernel(
        functools.partial(rotate_kernel, n, chips),
        [f32(each, width)] * n + [pltpu.VMEM((size, width), F32) for size in sizes[1:]],
        [WHOLE] * (chips + 1) + [FAR],
        (*from_chips, first, basis),
        [
            pltpu.VMEM((n * each, height), BF16),
            pltpu.VMEM((n * each, width), F32),
            pltpu.SemaphoreType.DMA((16,)),
        ],
        moved,
    )
    parts, (early, later, *rest) = results[:n], [
        pltpu.with_memory_space_constraint(x, pltpu.VMEM) for x in (first, *results[n:])
    ]
    parts = [parts[0]] + [along_cols(parts[s], s) for s in range(1, n)]
    pieces = list(
        kernel(turn_kernel, turned(sizes[0], width), [WHOLE] * (2 + len(rest)), (early, later, *rest), (), moved // 2)
    )
    pieces = [pltpu.with_memory_space_constraint(x, pltpu.VMEM) for x in pieces]
    normed, rotated = kernel(
        functools.partial(normed_kernel, n),
        [f32(each, width)] * 2,
        [WHOLE] * (n + 3 + len(pieces) + len(rest)),
        (moment, second, *parts, *pieces, later, *rest),
    )
    moment_new, second_new = kernel(
        moments_kernel, [f32(each, width)] * 2, [WHOLE] * 3, (moment, second, rotated), (), 8 * each * width * 4
    )
    blocks = [normed] + [along_cols(normed, s) for s in range(1, n)]
    pieces += list(kernel(turn_kernel, turned(sizes[1], width), [WHOLE] * (1 + len(rest)), (later, *rest), (), moved // 2))
    keep, send = kernel(
        functools.partial(back_kernel, n, len(pieces)),
        [f32(chips, four, height)] * 2,
        [WHOLE] * (n + len(pieces) + len(rest)),
        (*blocks, *pieces, *rest),
        [
            pltpu.VMEM((n * each, width), F32),
            pltpu.VMEM((2 * n * each, width), BF16),
            pltpu.VMEM((n * each, height), F32),
            pltpu.VMEM((2, width, height // 16), BF16),
            pltpu.VMEM((2, width, height // 16), BF16),
        ],
        moved,
    )
    got = along_rows(send, 1)
    halves = kernel(fold_kernel, [f32(four, height)] * chips, [WHOLE] * 2, (keep, got))
    update = halves[0]
    for s in range(1, chips):
        update = update + along_rows(halves[s], 2 * s)
    return (update, moment_new, second_new)


def solution(mesh):
    placed = (P("rows", "cols"), P("cols", "rows"), P("cols", "rows"), P("cols", "rows"))
    return jax.shard_map(
        step_on_device,
        mesh=mesh,
        in_specs=placed,
        out_specs=(P("rows", "cols"), P("cols", "rows"), P("cols", "rows")),
        check_vma=False,
    )
```

```python
import functools

import jax
import jax.numpy as jnp
from jax import lax
from jax.experimental import pallas as pl
from jax.experimental.pallas import tpu as pltpu
from jax.sharding import PartitionSpec as P

F32, BF16 = jnp.float32, jnp.bfloat16
WHOLE = pl.BlockSpec(memory_space=pltpu.VMEM)
FAR = pl.BlockSpec(memory_space=pltpu.HBM)
ANY = pl.BlockSpec(memory_space=pl.ANY)
LIMIT = 6 << 20
PARTS = (5, 5, 3, 3)


def f32(*shape):
    return jax.ShapeDtypeStruct(shape, F32)


def turned(rows, width):
    return [pltpu.VMEM((width, rows), BF16)] * 2


def kernel(body, outs, ins, args, scratch=(), moved=0):
    return pl.pallas_call(
        body,
        out_shape=outs,
        in_specs=ins,
        out_specs=jax.tree.map(lambda _: WHOLE, outs),
        scratch_shapes=scratch,
        cost_estimate=pl.CostEstimate(flops=0, bytes_accessed=moved, transcendentals=0) if moved else None,
        compiler_params=pltpu.CompilerParams(vmem_limit_bytes=LIMIT),
    )(*args)


def span(i, size):
    return pl.ds(pl.multiple_of(i * size, size), size)


def adam_moments(moment, second, rotated):
    moment_new = 0.9 * moment + 0.1 * rotated
    second_new = 0.95 * second + 0.05 * rotated * rotated
    normed = moment_new / (1.0 - 0.9**10) / (jnp.sqrt(second_new / (1.0 - 0.95**10)) + 1e-08)
    return (moment_new, second_new, normed)


def split(x):
    high = x.astype(BF16)
    return high, (x - high.astype(F32)).astype(BF16)


def stage_kernel(far, near, sem):
    copy = pltpu.make_async_copy(far, near, sem)
    copy.start()
    copy.wait()


def pack_kernel(own, got, out):
    even = lax.rem(lax.axis_index("rows"), 2) == 0
    own, got = own[...].astype(F32), got[...].astype(F32)
    out[...] = jnp.concatenate([jnp.where(even, own, got), jnp.where(even, got, own)], axis=0).astype(BF16)


def turn(take, high_ref, low_ref, row, rows):
    width = high_ref.shape[0]
    columns = min(width, 512)
    for j in range(width // columns):
        at = slice(j * columns, (j + 1) * columns)
        high, low = split(take(at))
        high_ref[at, pl.ds(row, rows)], low_ref[at, pl.ds(row, rows)] = high.T, low.T


def load_kernel(_, b_ref, near, sems):
    count = sems.shape[0]
    rows = near.shape[0] // count
    copies = [
        pltpu.make_async_copy(b_ref.at[pl.ds(i * rows, rows), :], near.at[pl.ds(i * rows, rows), :], sems.at[i])
        for i in range(count)
    ]
    for copy in copies:
        copy.start()
    for copy in copies:
        copy.wait()


def turn_kernel(b_ref, *refs):
    high_ref, low_ref = refs[-2:]
    rows = min(b_ref.shape[0], 256)
    for i in range(b_ref.shape[0] // rows):
        turn(lambda at, i=i: b_ref[i * rows : (i + 1) * rows, at], high_ref, low_ref, i * rows, rows)


def rotate_kernel(n, chips, *refs):
    blocks, (ready, b_ref), refs = refs[:chips], refs[chips : chips + 2], refs[chips + 2 :]
    outs, parts, (g_ref, total, sems) = refs[:n], refs[n : n + len(PARTS) - 1], refs[n + len(PARTS) - 1 :]
    width = ready.shape[1]
    rows, columns = b_ref.shape[0] // 16, min(width, 256)
    begins = [sum(PARTS[:p]) for p in range(len(PARTS))]

    def copy(p, i):
        k = begins[p] + i
        return pltpu.make_async_copy(b_ref.at[span(k, rows), :], parts[p - 1].at[span(i, rows), :], sems.at[k])

    end = len(PARTS) - 1
    half = rows // 2

    def half_copy(h):
        far = pl.ds(b_ref.shape[0] - rows + h * half, half)
        near = pl.ds((PARTS[end] - 1) * rows + h * half, half)
        return pltpu.make_async_copy(b_ref.at[far, :], parts[end - 1].at[near, :], sems.at[15 + h])

    for p in range(1, len(PARTS)):
        for i in range(PARTS[p] - (p == end)):
            copy(p, i).start()
    for h in range(2):
        half_copy(h).start()
    g_ref[...] = jnp.concatenate([block[...].astype(F32) for block in blocks], axis=0).astype(BF16)
    total[...] = jnp.zeros_like(total)
    for p, ref in enumerate((ready, *parts)):

        def tile(i, _, p=p, ref=ref):
            if p:
                copy(p, i).wait()
            g = g_ref[:, span(begins[p] + i, rows)]
            for j in range(width // columns):
                at = slice(j * columns, (j + 1) * columns)
                high, low = split(ref[span(i, rows), at])
                total[:, at] += jnp.dot(g, high, preferred_element_type=F32) + jnp.dot(
                    g, low, preferred_element_type=F32
                )
            return 0

        lax.fori_loop(0, PARTS[p] - (p == end), tile, 0)
    for h in range(2):
        half_copy(h).wait()
        begin = b_ref.shape[0] - rows + h * half
        near = (PARTS[end] - 1) * rows + h * half
        for j in range(width // columns):
            at = slice(j * columns, (j + 1) * columns)
            high, low = split(parts[end - 1][near : near + half, at])
            g = g_ref[:, begin : begin + half]
            total[:, at] += jnp.dot(g, high, preferred_element_type=F32) + jnp.dot(g, low, preferred_element_type=F32)
    pair = blocks[0].shape[0]
    chip = lax.axis_index("rows") // 2
    each = chips // n
    for s, out in enumerate(outs):
        place = (lax.axis_index("cols") ^ s) * each
        for i in range(each):
            out[i * pair : (i + 1) * pair, :] = total[span(chip ^ (place + i), pair), :]


def normed_kernel(n, m_ref, s_ref, *refs):
    parts, (normed, rotated) = refs[:n], refs[-2:]
    total = parts[0][...]
    for part in parts[1:]:
        total = total + part[...]
    rotated[...] = total
    normed[...] = adam_moments(m_ref[...], s_ref[...], total)[2]


def moments_kernel(m_ref, s_ref, rotated, moment_new, second_new):
    moment_new[...], second_new[...], _ = adam_moments(m_ref[...], s_ref[...], rotated[...])


def back_kernel(n, kept, *refs):
    blocks, pieces, rest = refs[:n], refs[n : n + kept], refs[n + kept : -7]
    keep, send, x_ref, x2_ref, o_ref, turned_high, turned_low = refs[-7:]
    each, rows = blocks[0].shape[0], x_ref.shape[0]
    for s, block in enumerate(blocks):
        x_ref[span(lax.axis_index("cols") ^ s, each), :] = block[...]
    high, low = split(x_ref[...])
    x2_ref[:rows, :], x2_ref[rows:, :] = high, low
    begins = [sum(PARTS[:p]) * o_ref.shape[1] // 16 for p in range(len(PARTS) + 1)]

    size = o_ref.shape[1] // 16

    def multiply(to, high, low):
        first = jnp.dot(x2_ref[...], high, preferred_element_type=F32)
        second = jnp.dot(x2_ref[:rows, :], low, preferred_element_type=F32)
        o_ref[:, to : to + size] = first[:rows] + first[rows:] + second

    ready = [
        (begins[p] + i * size, high, low, i)
        for p, (high, low) in enumerate(zip(pieces[::2], pieces[1::2]))
        for i in range(PARTS[p])
    ]
    waiting = [
        (begins[p] + i * size, ref, i) for p, ref in enumerate(rest, len(pieces) // 2) for i in range(PARTS[p])
    ]
    slots = turned_high.shape[0]
    for k, (_, ref, i) in enumerate(waiting):
        turn(lambda at, ref=ref, i=i: ref[i * size : (i + 1) * size, at], turned_high.at[k % slots], turned_low.at[k % slots], 0, size)
        for to, high, low, j in ready[k * len(ready) // len(waiting) : (k + 1) * len(ready) // len(waiting)]:
            multiply(to, high[:, j * size : (j + 1) * size], low[:, j * size : (j + 1) * size])
        if k:
            multiply(waiting[k - 1][0], turned_high[(k - 1) % slots], turned_low[(k - 1) % slots])
    multiply(waiting[-1][0], turned_high[(len(waiting) - 1) % slots], turned_low[(len(waiting) - 1) % slots])
    odd = lax.rem(lax.axis_index("rows"), 2) == 1
    chips, four, height = keep.shape
    whole = o_ref[...].reshape(chips, 2, four, height)
    keep[...] = jnp.where(odd, whole[:, 1], whole[:, 0])
    send[...] = jnp.where(odd, whole[:, 0], whole[:, 1])


def fold_kernel(keep, got, *outs):
    chip = lax.axis_index("rows") // 2
    total = keep[...] + got[...]
    for s, out in enumerate(outs):
        block = total[0]
        for i in range(1, len(outs)):
            block = jnp.where((chip ^ s) == i, total[i], block)
        out[...] = block


def step_on_device(gradient, basis, moment, second):
    n, m = lax.axis_size("cols"), lax.axis_size("rows")
    chips = m // 2
    each, width = moment.shape
    four, height = gradient.shape
    sizes = [share * height // 16 for share in PARTS]
    moved = height * width * 4

    def along(x, axis, size, s):
        return lax.ppermute(x, axis, [(i, i ^ s) for i in range(size)])

    def along_rows(x, s):
        return along(x, "rows", m, s)

    def along_cols(x, s):
        return along(x, "cols", n, s)

    basis = pltpu.with_memory_space_constraint(basis, pltpu.HBM)
    partner = along_rows(gradient, 1)
    own = kernel(
        stage_kernel,
        pltpu.VMEM(gradient.shape, BF16),
        [FAR],
        (pltpu.with_memory_space_constraint(gradient, pltpu.HBM),),
        [pltpu.SemaphoreType.DMA],
        four * height * 4,
    )
    own = kernel(pack_kernel, jax.ShapeDtypeStruct((2 * four, height), BF16), [WHOLE] * 2, (own, partner))
    from_chips = [own] + [along_rows(own, 2 * s) for s in range(1, chips)]
    first = kernel(
        load_kernel,
        pltpu.VMEM((sizes[0], width), F32),
        [ANY, FAR],
        (own, basis),
        [pltpu.SemaphoreType.DMA((4,))],
        moved // 2,
    )
    results = kernel(
        functools.partial(rotate_kernel, n, chips),
        [f32(each, width)] * n + [pltpu.VMEM((size, width), F32) for size in sizes[1:]],
        [WHOLE] * (chips + 1) + [FAR],
        (*from_chips, first, basis),
        [
            pltpu.VMEM((n * each, height), BF16),
            pltpu.VMEM((n * each, width), F32),
            pltpu.SemaphoreType.DMA((17,)),
        ],
        moved,
    )
    parts, (early, later, *rest) = results[:n], [
        pltpu.with_memory_space_constraint(x, pltpu.VMEM) for x in (first, *results[n:])
    ]
    parts = [parts[0]] + [along_cols(parts[s], s) for s in range(1, n)]
    pieces = list(
        kernel(turn_kernel, turned(sizes[0], width), [WHOLE] * (2 + len(rest)), (early, later, *rest), (), moved // 2)
    )
    pieces = [pltpu.with_memory_space_constraint(x, pltpu.VMEM) for x in pieces]
    normed, rotated = kernel(
        functools.partial(normed_kernel, n),
        [f32(each, width)] * 2,
        [WHOLE] * (n + 3 + len(pieces) + len(rest)),
        (moment, second, *parts, *pieces, later, *rest),
    )
    moment_new, second_new = kernel(
        moments_kernel, [f32(each, width)] * 2, [WHOLE] * 3, (moment, second, rotated), (), 8 * each * width * 4
    )
    blocks = [normed] + [along_cols(normed, s) for s in range(1, n)]
    pieces += list(kernel(turn_kernel, turned(sizes[1], width), [WHOLE] * (1 + len(rest)), (later, *rest), (), moved // 2))
    keep, send = kernel(
        functools.partial(back_kernel, n, len(pieces)),
        [f32(chips, four, height)] * 2,
        [WHOLE] * (n + len(pieces) + len(rest)),
        (*blocks, *pieces, *rest),
        [
            pltpu.VMEM((n * each, width), F32),
            pltpu.VMEM((2 * n * each, width), BF16),
            pltpu.VMEM((n * each, height), F32),
            pltpu.VMEM((2, width, height // 16), BF16),
            pltpu.VMEM((2, width, height // 16), BF16),
        ],
        moved,
    )
    got = along_rows(send, 1)
    halves = kernel(fold_kernel, [f32(four, height)] * chips, [WHOLE] * 2, (keep, got))
    update = halves[0]
    for s in range(1, chips):
        update = update + along_rows(halves[s], 2 * s)
    return (update, moment_new, second_new)


def solution(mesh):
    placed = (P("rows", "cols"), P("cols", "rows"), P("cols", "rows"), P("cols", "rows"))
    return jax.shard_map(
        step_on_device,
        mesh=mesh,
        in_specs=placed,
        out_specs=(P("rows", "cols"), P("cols", "rows"), P("cols", "rows")),
        check_vma=False,
    )
```
